32 devices in a mesh: blk: 8 (over y, x, core), uly: 4 (over z).
Axes of the slice: x: 2, y: 2, z: 4, core: 2. Of those that a mesh axis runs over, the one named last changes fastest.
Arguments:
- qkv: bfloat16 [2048, 3, 3072], P(('blk', 'uly')), may hold values from -9 to 9
Outputs:
- attended: float32 [2048, 3072], P('blk', 'uly')
- log_total: float32 [24, 2048], P('uly', 'blk')
The draws below stay inside these ranges and needn't reach their ends.
All inputs are finite; a program needn't handle non-finite values.
Results may differ from the reference program's by a relative error of at most 0.0027.
Values may be sent and summed in bfloat16 or wider, within the bound.
No kernel may reach another device: no remote copies, remote signals or barrier semaphores. Data moves between devices by JAX's collectives and lax.ppermute only.
A program may use at most 64 MiB of HBM per device.

```python
import math
import jax
import jax.numpy as jnp
from jax import lax

HEADS = 24
HEAD_DIM = 128
TOKENS = 2048
N_BLK = 8


def draw_qkv(key, part):
    first = jax.random.fold_in(jax.random.fold_in(key, 11), 0)
    width = HEADS * HEAD_DIM
    values = jnp.clip(jax.random.normal(first, (TOKENS, 3, width), jnp.float32), -6.0, 6.0)
    return values.astype(jnp.bfloat16)


def setup_inputs(seed: int = 0) -> dict:
    streams_of = jax.random.split(jax.random.key(seed), 2)
    return {
        "qkv": draw_qkv(jax.random.fold_in(streams_of[1], 71), 0),
    }


def block_scores(query_rows, key_rows, temper):
    return jnp.einsum('rhd,khd->hrk', query_rows, key_rows) * temper

def rounded(weights):
    return lax.optimization_barrier(weights.astype(jnp.bfloat16)).astype(jnp.float32)

def reference(qkv):
    block_len = TOKENS // N_BLK
    temper = 1.0 / math.sqrt(HEAD_DIM)
    shaped = qkv.reshape(N_BLK, block_len, 3, HEADS, HEAD_DIM)
    earlier = jnp.roll(shaped[:, :, 1:], 1, axis=0)

    def per_block(pieces):
        current, before = pieces
        current = current.astype(jnp.float32)
        before = before.astype(jnp.float32)
        queries = current[:, 0]
        scores = block_scores(queries, current[:, 1], temper)
        top = lax.optimization_barrier(jnp.max(scores, axis=2))
        weights = jnp.exp(scores - top[:, :, None])
        total = lax.optimization_barrier(jnp.sum(weights, axis=2))
        accum = jnp.einsum('hrk,khd->hrd', rounded(weights), current[:, 2])
        scores = block_scores(queries, before[:, 0], temper)
        newtop = jnp.maximum(top, lax.optimization_barrier(jnp.max(scores, axis=2)))
        factor = jnp.exp(top - newtop)
        weights = jnp.exp(scores - newtop[:, :, None])
        total = total * factor + lax.optimization_barrier(jnp.sum(weights, axis=2))
        accum = accum * factor[:, :, None] + jnp.einsum('hrk,khd->hrd', rounded(weights), before[:, 1])
        return (accum / total[:, :, None], newtop + jnp.log(total))
    attended, logs = lax.map(per_block, (shaped, earlier))
    attended = jnp.transpose(attended, (0, 2, 1, 3)).reshape(TOKENS, HEADS * HEAD_DIM)
    log_total = jnp.transpose(logs, (1, 0, 2)).reshape(HEADS, TOKENS)
    return (attended, log_total)
```

```python
import functools
import math

import jax
import jax.numpy as jnp
from jax import lax
from jax.experimental import pallas as pl
from jax.experimental.pallas import tpu as pltpu
from jax.sharding import PartitionSpec as P

HEAD_DIM = 128


def shift(value, axis, steps):
    count = lax.axis_size(axis)
    return lax.ppermute(value, axis, [(i, (i + steps) % count) for i in range(count)])


def attend_kernel(count, heads, rows, *refs):
    slot = refs[0]
    ins = refs[1 : 1 + 3 * count]
    out, log_out = refs[1 + 3 * count : 3 + 3 * count]
    q_all, own, prev, stat, sem = refs[3 + 3 * count :]
    piece = ins[0].shape[0]
    copies = []
    for i in range(count):
        start = pl.multiple_of(slot[i] * piece, piece)
        copies.append(pltpu.make_async_copy(ins[i], q_all.at[pl.ds(start, piece)], sem.at[0]))
        fixed = pl.ds(i * piece, piece)
        copies.append(pltpu.make_async_copy(ins[count + i], own.at[:, fixed], sem.at[1]))
        copies.append(pltpu.make_async_copy(ins[2 * count + i], prev.at[:, fixed], sem.at[2]))
    for copy in copies:
        copy.start()
    for copy in copies:
        copy.wait()
    temper = 1.0 / math.sqrt(HEAD_DIM)
    block_len = q_all.shape[0]
    contract = (((1,), (1,)), ((), ()))

    for r in range(block_len // rows):
        span = slice(r * rows, (r + 1) * rows)
        lane = lax.broadcasted_iota(jnp.int32, (rows, HEAD_DIM), 1)
        logs = jnp.zeros((rows, HEAD_DIM), jnp.float32)
        for h in range(heads):
            cols = slice(h * HEAD_DIM, (h + 1) * HEAD_DIM)
            query = q_all[span, cols]
            s0 = lax.dot_general(query, own[0, :, cols], contract, preferred_element_type=jnp.float32) * temper
            s1 = lax.dot_general(query, prev[0, :, cols], contract, preferred_element_type=jnp.float32) * temper
            top = jnp.max(s0, axis=1, keepdims=True)
            newtop = jnp.maximum(top, jnp.max(s1, axis=1, keepdims=True))
            w0 = jnp.exp(s0 - top)
            w1 = jnp.exp(s1 - newtop)
            factor = jnp.exp(top - newtop)
            total = jnp.sum(w0, axis=1, keepdims=True) * factor + jnp.sum(w1, axis=1, keepdims=True)
            a0 = jnp.dot(w0.astype(jnp.bfloat16), own[1, :, cols], preferred_element_type=jnp.float32)
            a1 = jnp.dot(w1.astype(jnp.bfloat16), prev[1, :, cols], preferred_element_type=jnp.float32)
            out[span, cols] = (a0 * factor + a1) / total
            logs = jnp.where(lane == h, newtop + jnp.log(total), logs)
        stat[:, span] = logs.T
    log_out[...] = stat[:heads, :]


def attend(slots, queries, own, prev, block_len, width):
    count = len(queries)
    heads = width // HEAD_DIM
    rows = math.gcd(block_len, 256)
    flops = 8 * block_len * block_len * width
    return pl.pallas_call(
        functools.partial(attend_kernel, count, heads, rows),
        out_shape=(
            jax.ShapeDtypeStruct((block_len, width), jnp.float32),
            jax.ShapeDtypeStruct((heads, block_len), jnp.float32),
        ),
        in_specs=[pl.BlockSpec(memory_space=pltpu.SMEM)]
        + [pl.BlockSpec(memory_space=pl.ANY)] * (3 * count),
        out_specs=(pl.BlockSpec(memory_space=pltpu.VMEM), pl.BlockSpec(memory_space=pltpu.VMEM)),
        scratch_shapes=[
            pltpu.VMEM((block_len, width), jnp.bfloat16),
            pltpu.VMEM((2, block_len, width), jnp.bfloat16),
            pltpu.VMEM((2, block_len, width), jnp.bfloat16),
            pltpu.VMEM((HEAD_DIM, block_len), jnp.float32),
            pltpu.SemaphoreType.DMA((3,)),
        ],
        compiler_params=pltpu.CompilerParams(vmem_limit_bytes=48 << 20),
        cost_estimate=pl.CostEstimate(
            flops=flops, bytes_accessed=14 * block_len * width, transcendentals=2 * block_len * block_len * heads
        ),
        name="attend",
    )(slots, *queries, *own, *prev)


def shards(qkv):
    count = lax.axis_size("uly")
    me = lax.axis_index("uly")
    width = qkv.shape[2] // count
    block_len = qkv.shape[0] * count
    planes = jnp.transpose(qkv, (1, 0, 2))

    def cut(first, last, k):
        return lax.dynamic_slice_in_dim(planes[first:last], lax.rem(me + k, count) * width, width, 2)

    own = [cut(1, 3, 0)]
    prev = [shift(own[0], "blk", 1)]
    queries = [cut(0, 1, 0)[0]]
    for k in range(1, count):
        own.append(shift(cut(1, 3, k), "uly", k))
    for k in range(1, count):
        prev.append(shift(own[k], "blk", 1))
    for k in range(1, count):
        queries.append(shift(cut(0, 1, k)[0], "uly", k))
    slots = lax.rem(me - jnp.arange(count, dtype=jnp.int32) + count, count)
    return attend(slots, queries, own, prev, block_len, width)


def solution(mesh):
    placed = (P(("blk", "uly"), None, None),)
    return jax.shard_map(
        shards,
        mesh=mesh,
        in_specs=placed,
        out_specs=(P("blk", "uly"), P("uly", "blk")),
        check_vma=False,
    )
```

```python
import functools
import math

import jax
import jax.numpy as jnp
from jax import lax
from jax.experimental import pallas as pl
from jax.experimental.pallas import tpu as pltpu
from jax.sharding import PartitionSpec as P

HEAD_DIM = 128
TEMPER = 1.0 / math.sqrt(HEAD_DIM)


def shift(value, axis, steps):
    count = lax.axis_size(axis)
    return lax.ppermute(value, axis, [(i, (i + steps) % count) for i in range(count)])


def after(value, *others):
    return lax.optimization_barrier((value, *others))[0]


def stack(parts):
    return parts[0] if len(parts) == 1 else jnp.concatenate(parts, axis=0)


def attend_kernel(count, heads, group, *refs):
    me = lax.axis_index("uly")
    refs = (None, *refs)
    home = refs[1]
    fulls = refs[1:3]
    pairs = refs[3 : 1 + count]
    singles = refs[1 + count : 2 * count - 1]
    prev_home, prev_early, *prev_last = refs[2 * count - 1 : 2 * count + 3]
    out, log_out, result, stat, turned, sem = refs[2 * count + 3 :]
    piece = home.shape[1]
    contract = (((1,), (1,)), ((), ()))

    def rows_of(k):
        slot = jnp.where(me < k, me + (count - k), me - k)
        return pl.ds(pl.multiple_of(slot * piece, piece), piece)

    def queries(k, cols):
        return fulls[k][0, :, cols] if k < 2 else singles[k - 2][:, cols]

    def own(which, cols):
        return stack(
            [ref[1 + which, :, cols] for ref in fulls] + [ref[which, :, cols] for ref in pairs]
        )

    def prev(which, cols):
        parts = [prev_early[i, which, :, cols] for i in range(count - 2)]
        return stack([prev_home[which, :, cols]] + parts + [prev_last[which][:, cols]])

    lane = lax.broadcasted_iota(jnp.int32, (group * piece, HEAD_DIM), 1)
    logs = [jnp.zeros((group * piece, HEAD_DIM), jnp.float32) for _ in range(count // group)]
    copies = []
    for h in range(heads):
        cols = slice(h * HEAD_DIM, (h + 1) * HEAD_DIM)
        own_keys, own_values = own(0, cols), own(1, cols)
        prev_keys, prev_values = prev(0, cols), prev(1, cols)
        for g in range(count // group):
            query = stack([queries(k, cols) for k in range(g * group, (g + 1) * group)])
            s0 = lax.dot_general(query, own_keys, contract, preferred_element_type=jnp.float32)
            s1 = lax.dot_general(query, prev_keys, contract, preferred_element_type=jnp.float32)
            top = jnp.max(s0, axis=1, keepdims=True)
            newtop = jnp.maximum(top, jnp.max(s1, axis=1, keepdims=True))
            scale = TEMPER * math.log2(math.e)
            w0 = jnp.exp2((s0 - top) * scale)
            w1 = jnp.exp2((s1 - newtop) * scale)
            factor = jnp.exp2((top - newtop) * scale)
            total = jnp.sum(w0, axis=1, keepdims=True) * factor + jnp.sum(w1, axis=1, keepdims=True)
            a0 = jnp.dot(w0.astype(jnp.bfloat16), own_values, preferred_element_type=jnp.float32)
            a1 = jnp.dot(w1.astype(jnp.bfloat16), prev_values, preferred_element_type=jnp.float32)
            normed = (a0 * factor + a1) / total
            logs[g] = jnp.where(lane == h, newtop * TEMPER + jnp.log(total), logs[g])
            for i in range(group):
                result[rows_of(g * group + i), cols] = normed[i * piece : (i + 1) * piece]
        copies.append(pltpu.make_async_copy(result.at[:, cols], out.at[:, cols], sem))
        copies[-1].start()
    for g in range(count // group):
        for i in range(group):
            stat[rows_of(g * group + i), :] = logs[g][i * piece : (i + 1) * piece]
    turned[...] = stat[...].T[:heads, :]
    copies.append(pltpu.make_async_copy(turned, log_out, sem))
    copies[-1].start()
    for copy in copies:
        copy.wait()


def attend(fulls, pairs, singles, prevs, block_len, width):
    count = len(pairs) + 2
    heads = width // HEAD_DIM
    group = math.gcd(count, 4)
    in_vmem = pl.BlockSpec(memory_space=pltpu.VMEM)
    return pl.pallas_call(
        functools.partial(attend_kernel, count, heads, group),
        out_shape=(
            jax.ShapeDtypeStruct((block_len, width), jnp.float32),
            jax.ShapeDtypeStruct((heads, block_len), jnp.float32),
        ),
        in_specs=[in_vmem] * (2 * count + 2),
        out_specs=(pl.BlockSpec(memory_space=pl.ANY), pl.BlockSpec(memory_space=pl.ANY)),
        scratch_shapes=[
            pltpu.VMEM((block_len, width), jnp.float32),
            pltpu.VMEM((block_len, HEAD_DIM), jnp.float32),
            pltpu.VMEM((heads, block_len), jnp.float32),
            pltpu.SemaphoreType.DMA(()),
        ],
        compiler_params=pltpu.CompilerParams(vmem_limit_bytes=48 << 20),
        cost_estimate=pl.CostEstimate(
            flops=8 * block_len * block_len * width,
            bytes_accessed=14 * block_len * width,
            transcendentals=2 * block_len * block_len * heads,
        ),
        name="attend",
    )(*fulls, *pairs, *singles, *prevs)


def shards(qkv):
    count = lax.axis_size("uly")
    me = lax.axis_index("uly")
    tokens, planes_count, width = qkv.shape[0], qkv.shape[1], qkv.shape[2] // count
    planes = jnp.transpose(qkv, (1, 0, 2))

    def cut(first, last, k):
        start = jnp.where(me + k < count, me + k, me + k - count) * width
        return lax.dynamic_slice(planes, (first, 0, start), (last - first, tokens, width))

    home = cut(0, planes_count, 0)
    first = shift(cut(0, planes_count, 1), "uly", 1)
    prevs = [shift(home[1:], "blk", 1)]
    last = count // 2
    pairs, singles = [], []
    for k in range(2, count):
        pair, single = cut(1, planes_count, k), cut(0, 1, k)[0]
        pairs.append(shift(after(pair, prevs[0]) if k == last else pair, "uly", k))
        singles.append(shift(after(single, prevs[0]), "uly", k))
    early = [first[1:]] + [pair for k, pair in enumerate(pairs, 2) if k != last]
    prevs.append(shift(jnp.stack(early), "blk", 1))
    prevs += [shift(pairs[last - 2][i], "blk", 1) for i in range(2)]
    return attend([home, first], pairs, singles, prevs, tokens * count, width)


def solution(mesh):
    placed = (P(("blk", "uly"), None, None),)
    return jax.shard_map(
        shards,
        mesh=mesh,
        in_specs=placed,
        out_specs=(P("blk", "uly"), P("uly", "blk")),
        check_vma=False,
    )
```

```python
import functools
import math

import jax
import jax.numpy as jnp
from jax import lax
from jax.experimental import pallas as pl
from jax.experimental.pallas import tpu as pltpu
from jax.sharding import PartitionSpec as P

HEAD_DIM = 128
TEMPER = 1.0 / math.sqrt(HEAD_DIM)
SCALE = TEMPER * math.log2(math.e)
CONTRACT = (((1,), (1,)), ((), ()))


def shift(value, axis, steps):
    count = lax.axis_size(axis)
    return lax.ppermute(value, axis, [(i, (i + steps) % count) for i in range(count)])


def after(value, *others):
    return lax.optimization_barrier((value, *others))[0]


def stack(parts):
    return parts[0] if len(parts) == 1 else jnp.concatenate(parts, axis=0)


def own_kernel(count, heads, group, *refs):
    fulls = refs[:2]
    pairs = refs[2:count]
    singles = refs[count : 2 * count - 2]
    accum, top_out, total_out = refs[2 * count - 2 :]
    piece = fulls[0].shape[1]
    rows = group * piece

    def queries(k, cols):
        return fulls[k][0, :, cols] if k < 2 else singles[k - 2][:, cols]

    def own(which, cols):
        return stack(
            [ref[1 + which, :, cols] for ref in fulls] + [ref[which, :, cols] for ref in pairs]
        )

    for h in range(heads):
        cols = slice(h * HEAD_DIM, (h + 1) * HEAD_DIM)
        keys, values = own(0, cols), own(1, cols)
        for g in range(count // group):
            query = stack([queries(k, cols) for k in range(g * group, (g + 1) * group)])
            scores = lax.dot_general(query, keys, CONTRACT, preferred_element_type=jnp.float32)
            top = jnp.max(scores, axis=1, keepdims=True)
            weights = jnp.exp2((scores - top) * SCALE)
            total = jnp.sum(weights, axis=1, keepdims=True)
            span = slice(g * rows, (g + 1) * rows)
            accum[span, cols] = jnp.dot(
                weights.astype(jnp.bfloat16), values, preferred_element_type=jnp.float32
            )
            top_out[span, cols] = jnp.broadcast_to(top, (rows, HEAD_DIM))
            total_out[span, cols] = jnp.broadcast_to(total, (rows, HEAD_DIM))


def prev_kernel(count, heads, group, *refs):
    me = lax.axis_index("uly")
    fulls = refs[:2]
    singles = refs[2:count]
    prev_home, prev_early, *prev_last = refs[count : count + 4]
    accum, top_in, total_in, out, log_out, result, stat, turned, sem = refs[count + 4 :]
    piece = fulls[0].shape[1]
    rows = group * piece

    def rows_of(k):
        slot = jnp.where(me < k, me + (count - k), me - k)
        return pl.ds(pl.multiple_of(slot * piece, piece), piece)

    def queries(k, cols):
        return fulls[k][0, :, cols] if k < 2 else singles[k - 2][:, cols]

    def prev(which, cols):
        parts = [prev_early[i, which, :, cols] for i in range(count - 2)]
        return stack([prev_home[which, :, cols]] + parts + [prev_last[which][:, cols]])

    lane = lax.broadcasted_iota(jnp.int32, (rows, HEAD_DIM), 1)
    logs = [jnp.zeros((rows, HEAD_DIM), jnp.float32)] * (count // group)
    copies = []
    for h in range(heads):
        cols = slice(h * HEAD_DIM, (h + 1) * HEAD_DIM)
        keys, values = prev(0, cols), prev(1, cols)
        for g in range(count // group):
            span = slice(g * rows, (g + 1) * rows)
            query = stack([queries(k, cols) for k in range(g * group, (g + 1) * group)])
            scores = lax.dot_general(query, keys, CONTRACT, preferred_element_type=jnp.float32)
            top, total = top_in[span, cols], total_in[span, cols]
            newtop = jnp.maximum(top, jnp.max(scores, axis=1, keepdims=True))
            wide = jnp.concatenate([newtop] * (scores.shape[1] // HEAD_DIM), axis=1)
            weights = jnp.exp2((scores - wide) * SCALE)
            factor = jnp.exp2((top - newtop) * SCALE)
            total = total * factor + jnp.sum(weights, axis=1, keepdims=True)
            added = jnp.dot(weights.astype(jnp.bfloat16), values, preferred_element_type=jnp.float32)
            normed = (accum[span, cols] * factor + added) / total
            logs[g] = jnp.where(lane == h, newtop * TEMPER + jnp.log(total), logs[g])
            for i in range(group):
                result[rows_of(g * group + i), cols] = normed[i * piece : (i + 1) * piece]
        copies.append(pltpu.make_async_copy(result.at[:, cols], out.at[:, cols], sem))
        copies[-1].start()
    for g in range(count // group):
        for i in range(group):
            stat[rows_of(g * group + i), :] = logs[g][i * piece : (i + 1) * piece]
    turned[...] = stat[...].T[:heads, :]
    copies.append(pltpu.make_async_copy(turned, log_out, sem))
    copies[-1].start()
    for copy in copies:
        copy.wait()


def cost(block_len, width):
    return pl.CostEstimate(
        flops=4 * block_len * block_len * width,
        bytes_accessed=7 * block_len * width,
        transcendentals=block_len * block_len * width // HEAD_DIM,
    )


def attend(fulls, pairs, singles, prevs, block_len, width):
    count = len(pairs) + 2
    heads = width // HEAD_DIM
    group = math.gcd(count, 4)
    in_vmem = pl.BlockSpec(memory_space=pltpu.VMEM)
    whole = jax.ShapeDtypeStruct((block_len, width), jnp.float32)
    running = pl.pallas_call(
        functools.partial(own_kernel, count, heads, group),
        out_shape=(whole, whole, whole),
        in_specs=[in_vmem] * (2 * count - 2),
        out_specs=(in_vmem,) * 3,
        compiler_params=pltpu.CompilerParams(vmem_limit_bytes=24 << 20),
        cost_estimate=cost(block_len, width),
        name="attend_own",
    )(*fulls, *pairs, *singles)
    return pl.pallas_call(
        functools.partial(prev_kernel, count, heads, group),
        out_shape=(whole, jax.ShapeDtypeStruct((heads, block_len), jnp.float32)),
        in_specs=[in_vmem] * (count + 7),
        out_specs=(pl.BlockSpec(memory_space=pl.ANY), pl.BlockSpec(memory_space=pl.ANY)),
        scratch_shapes=[
            pltpu.VMEM((block_len, width), jnp.float32),
            pltpu.VMEM((block_len, HEAD_DIM), jnp.float32),
            pltpu.VMEM((heads, block_len), jnp.float32),
            pltpu.SemaphoreType.DMA(()),
        ],
        compiler_params=pltpu.CompilerParams(vmem_limit_bytes=24 << 20),
        cost_estimate=cost(block_len, width),
        name="attend_prev",
    )(*fulls, *singles, *prevs, *running)


def shards(qkv):
    count = lax.axis_size("uly")
    me = lax.axis_index("uly")
    tokens, planes_count, width = qkv.shape[0], qkv.shape[1], qkv.shape[2] // count
    planes = jnp.transpose(qkv, (1, 0, 2))

    def cut(first, last, k):
        start = jnp.where(me + k < count, me + k, me + k - count) * width
        return lax.dynamic_slice(planes, (first, 0, start), (last - first, tokens, width))

    home = cut(0, planes_count, 0)
    first = shift(cut(0, planes_count, 1), "uly", 1)
    prevs = [shift(home[1:], "blk", 1)]
    last = count // 2
    pairs, singles = [], []
    for k in range(2, count):
        pair, single = cut(1, planes_count, k), cut(0, 1, k)[0]
        pairs.append(shift(after(pair, prevs[0]) if k == last else pair, "uly", k))
        singles.append(shift(after(single, prevs[0]), "uly", k))
    early = [first[1:]] + [pair for k, pair in enumerate(pairs, 2) if k != last]
    prevs.append(shift(jnp.stack(early), "blk", 1))
    prevs += [shift(pairs[last - 2][i], "blk", 1) for i in range(2)]
    return attend([home, first], pairs, singles, prevs, tokens * count, width)


def solution(mesh):
    placed = (P(("blk", "uly"), None, None),)
    return jax.shard_map(
        shards,
        mesh=mesh,
        in_specs=placed,
        out_specs=(P("blk", "uly"), P("uly", "blk")),
        check_vma=False,
    )
```

```python
import functools
import math

import jax
import jax.numpy as jnp
from jax import lax
from jax.experimental import pallas as pl
from jax.experimental.pallas import tpu as pltpu
from jax.sharding import PartitionSpec as P

HEAD_DIM = 128
TEMPER = 1.0 / math.sqrt(HEAD_DIM)
SCALE = TEMPER * math.log2(math.e)
CONTRACT = (((1,), (1,)), ((), ()))


def shift(value, axis, steps):
    count = lax.axis_size(axis)
    return lax.ppermute(value, axis, [(i, (i + steps) % count) for i in range(count)])


def after(value, *others):
    return lax.optimization_barrier((value, *others))[0]


def stack(parts):
    return parts[0] if len(parts) == 1 else jnp.concatenate(parts, axis=0)


def own_kernel(count, heads, group, *refs):
    fulls = refs[:2]
    pairs = refs[2:count]
    singles = refs[count : 2 * count - 2]
    accum, top_out, total_out = refs[2 * count - 2 :]
    piece = fulls[0].shape[1]
    rows = group * piece

    def queries(k, cols):
        return fulls[k][0, :, cols] if k < 2 else singles[count - 1 - k][:, cols]

    def own(which, cols):
        return stack(
            [ref[1 + which, :, cols] for ref in fulls] + [ref[which, :, cols] for ref in pairs]
        )

    for h in range(heads):
        cols = slice(h * HEAD_DIM, (h + 1) * HEAD_DIM)
        keys, values = own(0, cols), own(1, cols)
        for g in range(count // group):
            query = stack([queries(k, cols) for k in range(g * group, (g + 1) * group)])
            scores = lax.dot_general(query, keys, CONTRACT, preferred_element_type=jnp.float32)
            top = jnp.max(scores, axis=1, keepdims=True)
            weights = jnp.exp2((scores - top) * SCALE)
            total = jnp.sum(weights, axis=1, keepdims=True)
            span = slice(g * rows, (g + 1) * rows)
            accum[span, cols] = jnp.dot(
                weights.astype(jnp.bfloat16), values, preferred_element_type=jnp.float32
            )
            top_out[span, cols] = jnp.broadcast_to(top, (rows, HEAD_DIM))
            total_out[span, cols] = jnp.broadcast_to(total, (rows, HEAD_DIM))


def prev_kernel(count, heads, group, *refs):
    me = lax.axis_index("uly")
    fulls = refs[:2]
    singles = refs[2:count]
    prev_home, prev_early, *prev_last = refs[count : count + 4]
    accum, top_in, total_in, out, log_out, result, stat, turned, sem = refs[count + 4 :]
    piece = fulls[0].shape[1]
    rows = group * piece

    def rows_of(k):
        slot = jnp.where(me < k, me + (count - k), me - k)
        return pl.ds(pl.multiple_of(slot * piece, piece), piece)

    def queries(k, cols):
        return fulls[k][0, :, cols] if k < 2 else singles[count - 1 - k][:, cols]

    def prev(which, cols):
        parts = [prev_early[i, which, :, cols] for i in range(count - 2)]
        return stack([prev_home[which, :, cols]] + parts + [prev_last[which][:, cols]])

    lane = lax.broadcasted_iota(jnp.int32, (rows, HEAD_DIM), 1)
    logs = [jnp.zeros((rows, HEAD_DIM), jnp.float32)] * (count // group)
    copies = []
    for h in range(heads):
        cols = slice(h * HEAD_DIM, (h + 1) * HEAD_DIM)
        keys, values = prev(0, cols), prev(1, cols)
        for g in range(count // group):
            span = slice(g * rows, (g + 1) * rows)
            query = stack([queries(k, cols) for k in range(g * group, (g + 1) * group)])
            scores = lax.dot_general(query, keys, CONTRACT, preferred_element_type=jnp.float32)
            top, total = top_in[span, cols], total_in[span, cols]
            newtop = jnp.maximum(top, jnp.max(scores, axis=1, keepdims=True))
            wide = jnp.concatenate([newtop] * (scores.shape[1] // HEAD_DIM), axis=1)
            weights = jnp.exp2((scores - wide) * SCALE)
            factor = jnp.exp2((top - newtop) * SCALE)
            total = total * factor + jnp.sum(weights, axis=1, keepdims=True)
            added = jnp.dot(weights.astype(jnp.bfloat16), values, preferred_element_type=jnp.float32)
            normed = (accum[span, cols] * factor + added) / total
            logs[g] = jnp.where(lane == h, newtop * TEMPER + jnp.log(total), logs[g])
            for i in range(group):
                result[rows_of(g * group + i), cols] = normed[i * piece : (i + 1) * piece]
        copies.append(pltpu.make_async_copy(result.at[:, cols], out.at[:, cols], sem))
        copies[-1].start()
    for g in range(count // group):
        for i in range(group):
            stat[rows_of(g * group + i), :] = logs[g][i * piece : (i + 1) * piece]
    turned[...] = stat[...].T[:heads, :]
    copies.append(pltpu.make_async_copy(turned, log_out, sem))
    copies[-1].start()
    for copy in copies:
        copy.wait()


def cost(block_len, width):
    return pl.CostEstimate(
        flops=4 * block_len * block_len * width,
        bytes_accessed=7 * block_len * width,
        transcendentals=block_len * block_len * width // HEAD_DIM,
    )


def attend(fulls, pairs, singles, prevs, block_len, width):
    count = len(pairs) + 2
    heads = width // HEAD_DIM
    group = math.gcd(count, 4)
    in_vmem = pl.BlockSpec(memory_space=pltpu.VMEM)
    whole = jax.ShapeDtypeStruct((block_len, width), jnp.float32)
    running = pl.pallas_call(
        functools.partial(own_kernel, count, heads, group),
        out_shape=(whole, whole, whole),
        in_specs=[in_vmem] * (2 * count - 2),
        out_specs=(in_vmem,) * 3,
        compiler_params=pltpu.CompilerParams(vmem_limit_bytes=24 << 20),
        cost_estimate=cost(block_len, width),
        name="attend_own",
    )(*fulls, *pairs, *reversed(singles))
    return pl.pallas_call(
        functools.partial(prev_kernel, count, heads, group),
        out_shape=(whole, jax.ShapeDtypeStruct((heads, block_len), jnp.float32)),
        in_specs=[in_vmem] * (count + 7),
        out_specs=(pl.BlockSpec(memory_space=pl.ANY), pl.BlockSpec(memory_space=pl.ANY)),
        scratch_shapes=[
            pltpu.VMEM((block_len, width), jnp.float32),
            pltpu.VMEM((block_len, HEAD_DIM), jnp.float32),
            pltpu.VMEM((heads, block_len), jnp.float32),
            pltpu.SemaphoreType.DMA(()),
        ],
        compiler_params=pltpu.CompilerParams(vmem_limit_bytes=24 << 20),
        cost_estimate=cost(block_len, width),
        name="attend_prev",
    )(*fulls, *reversed(singles), *prevs, *running)


def shards(qkv):
    count = lax.axis_size("uly")
    me = lax.axis_index("uly")
    tokens, planes_count, width = qkv.shape[0], qkv.shape[1], qkv.shape[2] // count
    planes = jnp.transpose(qkv, (1, 0, 2))

    def cut(first, last, k):
        start = jnp.where(me + k < count, me + k, me + k - count) * width
        return lax.dynamic_slice(planes, (first, 0, start), (last - first, tokens, width))

    home = cut(0, planes_count, 0)
    first = shift(cut(0, planes_count, 1), "uly", 1)
    prevs = [shift(home[1:], "blk", 1)]
    last = count // 2
    pairs, singles = [], []
    for k in range(2, count):
        pair, single = cut(1, planes_count, k), cut(0, 1, k)[0]
        pairs.append(shift(after(pair, prevs[0]) if k == last else pair, "uly", k))
        singles.append(shift(after(single, prevs[0]), "uly", k))
    early = [first[1:]] + [pair for k, pair in enumerate(pairs, 2) if k != last]
    prevs.append(shift(jnp.stack(early), "blk", 1))
    prevs += [shift(pairs[last - 2][i], "blk", 1) for i in range(2)]
    return attend([home, first], pairs, singles, prevs, tokens * count, width)


def solution(mesh):
    placed = (P(("blk", "uly"), None, None),)
    return jax.shard_map(
        shards,
        mesh=mesh,
        in_specs=placed,
        out_specs=(P("blk", "uly"), P("uly", "blk")),
        check_vma=False,
    )
```

```python
import functools
import math

import jax
import jax.numpy as jnp
from jax import lax
from jax.experimental import pallas as pl
from jax.experimental.pallas import tpu as pltpu
from jax.sharding import PartitionSpec as P

HEAD_DIM = 128
TEMPER = 1.0 / math.sqrt(HEAD_DIM)
SCALE = TEMPER * math.log2(math.e)
CONTRACT = (((1,), (1,)), ((), ()))


def shift(value, axis, steps):
    count = lax.axis_size(axis)
    return lax.ppermute(value, axis, [(i, (i + steps) % count) for i in range(count)])


def after(value, *others):
    return lax.optimization_barrier((value, *others))[0]


def stack(parts):
    return parts[0] if len(parts) == 1 else jnp.concatenate(parts, axis=0)


def own_kernel(order, heads, group, *refs):
    count = len(order)
    fulls = refs[:2]
    pairs = refs[2:count]
    singles = refs[count : 2 * count - 2]
    accum, top_out, total_out = refs[2 * count - 2 :]
    piece = fulls[0].shape[1]
    rows = group * piece

    def queries(k, cols):
        return fulls[k][0, :, cols] if k < 2 else singles[k - 2][:, cols]

    def own(which, cols):
        return stack(
            [ref[1 + which, :, cols] for ref in fulls] + [ref[which, :, cols] for ref in pairs]
        )

    for h in range(heads):
        cols = slice(h * HEAD_DIM, (h + 1) * HEAD_DIM)
        keys, values = own(0, cols), own(1, cols)
        for g in range(count // group):
            query = stack([queries(k, cols) for k in range(g * group, (g + 1) * group)])
            scores = lax.dot_general(query, keys, CONTRACT, preferred_element_type=jnp.float32)
            top = jnp.max(scores, axis=1, keepdims=True)
            weights = jnp.exp2((scores - top) * SCALE)
            total = jnp.sum(weights, axis=1, keepdims=True)
            span = slice(g * rows, (g + 1) * rows)
            accum[span, cols] = jnp.dot(
                weights.astype(jnp.bfloat16), values, preferred_element_type=jnp.float32
            )
            top_out[span, cols] = jnp.broadcast_to(top, (rows, HEAD_DIM))
            total_out[span, cols] = jnp.broadcast_to(total, (rows, HEAD_DIM))


def prev_weights_kernel(order, heads, group, *refs):
    count = len(order)
    me = lax.axis_index("uly")
    fulls = refs[:2]
    singles = refs[2:count]
    prev_home, prev_early, prev_last = refs[count : count + 3]
    accum, top_in, total_in, scaled, inverse, packed, turned, stat = refs[count + 3 :]
    piece = fulls[0].shape[1]
    rows = group * piece

    def rows_of(i):
        k = order[i]
        slot = jnp.where(me < k, me + (count - k), me - k)
        return pl.ds(pl.multiple_of(slot * piece, piece), piece)

    def queries(k, cols):
        return fulls[k][0, :, cols] if k < 2 else singles[k - 2][:, cols]

    lane = lax.broadcasted_iota(jnp.int32, (rows, HEAD_DIM), 1)
    logs = [jnp.zeros((rows, HEAD_DIM), jnp.float32)] * (count // group)
    for h in range(heads):
        cols = slice(h * HEAD_DIM, (h + 1) * HEAD_DIM)
        parts = [prev_early[i, 0, :, cols] for i in range(count - 2)]
        keys = stack([prev_home[0, :, cols]] + parts + [prev_last[:, cols]])
        wide = keys.shape[0]
        for g in range(count // group):
            span = slice(g * rows, (g + 1) * rows)
            query = stack([queries(k, cols) for k in range(g * group, (g + 1) * group)])
            scores = lax.dot_general(query, keys, CONTRACT, preferred_element_type=jnp.float32)
            top, total = top_in[span, cols], total_in[span, cols]
            newtop = jnp.maximum(top, jnp.max(scores, axis=1, keepdims=True))
            spread = jnp.concatenate([newtop] * (wide // HEAD_DIM), axis=1)
            weights = jnp.exp2((scores - spread) * SCALE)
            factor = jnp.exp2((top - newtop) * SCALE)
            total = total * factor + jnp.sum(weights, axis=1, keepdims=True)
            packed[span, h * wide : (h + 1) * wide] = weights.astype(jnp.bfloat16)
            recip = 1.0 / total
            inverse[span, cols] = recip
            scaled[span, cols] = accum[span, cols] * (factor * recip)
            logs[g] = jnp.where(lane == h, newtop * TEMPER + jnp.log(total), logs[g])
    for g in range(count // group):
        for i in range(group):
            stat[rows_of(g * group + i), :] = logs[g][i * piece : (i + 1) * piece]
    turned[...] = stat[...].T[:heads, :]


def prev_values_kernel(order, heads, group, *refs):
    count = len(order)
    me = lax.axis_index("uly")
    prev_home, prev_early, prev_last = refs[:3]
    scaled, inverse, packed, turned, out, log_out, result, sem = refs[3:]
    piece = prev_last.shape[0]
    rows = group * piece

    def rows_of(i):
        k = order[i]
        slot = jnp.where(me < k, me + (count - k), me - k)
        return pl.ds(pl.multiple_of(slot * piece, piece), piece)

    copies = [pltpu.make_async_copy(turned, log_out, sem)]
    copies[0].start()
    for h in range(heads):
        cols = slice(h * HEAD_DIM, (h + 1) * HEAD_DIM)
        parts = [prev_early[i, 1, :, cols] for i in range(count - 2)]
        values = stack([prev_home[1, :, cols]] + parts + [prev_last[:, cols]])
        wide = values.shape[0]
        for g in range(count // group):
            span = slice(g * rows, (g + 1) * rows)
            weights = packed[span, h * wide : (h + 1) * wide]
            added = jnp.dot(weights, values, preferred_element_type=jnp.float32)
            normed = scaled[span, cols] + added * inverse[span, cols]
            for i in range(group):
                result[rows_of(g * group + i), cols] = normed[i * piece : (i + 1) * piece]
        copies.append(pltpu.make_async_copy(result.at[:, cols], out.at[:, cols], sem))
        copies[-1].start()
    for copy in copies:
        copy.wait()


def cost(block_len, width):
    return pl.CostEstimate(
        flops=4 * block_len * block_len * width,
        bytes_accessed=7 * block_len * width,
        transcendentals=block_len * block_len * width // HEAD_DIM,
    )


def attend(order, fulls, pairs, singles, prevs, block_len, width):
    count = len(order)
    heads = width // HEAD_DIM
    group = math.gcd(count, 4)
    in_vmem = pl.BlockSpec(memory_space=pltpu.VMEM)
    whole = jax.ShapeDtypeStruct((block_len, width), jnp.float32)
    running = pl.pallas_call(
        functools.partial(own_kernel, order, heads, group),
        out_shape=(whole, whole, whole),
        in_specs=[in_vmem] * (2 * count - 2),
        out_specs=(in_vmem,) * 3,
        compiler_params=pltpu.CompilerParams(vmem_limit_bytes=24 << 20),
        cost_estimate=cost(block_len, width),
        name="attend_own",
    )(*fulls, *pairs, *singles)
    prev_home, prev_early, last_keys, last_values = prevs
    logs = jax.ShapeDtypeStruct((heads, block_len), jnp.float32)
    scaled, inverse, packed, turned = pl.pallas_call(
        functools.partial(prev_weights_kernel, order, heads, group),
        out_shape=(whole, whole, jax.ShapeDtypeStruct((block_len, heads * block_len), jnp.bfloat16), logs),
        in_specs=[in_vmem] * (count + 6),
        out_specs=(in_vmem,) * 4,
        scratch_shapes=[pltpu.VMEM((block_len, HEAD_DIM), jnp.float32)],
        compiler_params=pltpu.CompilerParams(vmem_limit_bytes=24 << 20),
        cost_estimate=cost(block_len, width),
        name="attend_prev_weights",
    )(*fulls, *singles, prev_home, prev_early, last_keys, *running)
    return pl.pallas_call(
        functools.partial(prev_values_kernel, order, heads, group),
        out_shape=(whole, logs),
        in_specs=[in_vmem] * 7,
        out_specs=(pl.BlockSpec(memory_space=pl.ANY),) * 2,
        scratch_shapes=[pltpu.VMEM((block_len, width), jnp.float32), pltpu.SemaphoreType.DMA(())],
        compiler_params=pltpu.CompilerParams(vmem_limit_bytes=24 << 20),
        cost_estimate=cost(block_len, width),
        name="attend_prev_values",
    )(prev_home, prev_early, last_values, scaled, inverse, packed, turned)


def shards(qkv):
    count = lax.axis_size("uly")
    me = lax.axis_index("uly")
    tokens, planes_count, width = qkv.shape[0], qkv.shape[1], qkv.shape[2] // count
    planes = jnp.transpose(qkv, (1, 0, 2))

    def cut(first, last, k):
        start = jnp.where(me + k < count, me + k, me + k - count) * width
        return lax.dynamic_slice(planes, (first, 0, start), (last - first, tokens, width))

    mid = count // 2
    steps = [k for k in range(2, count) if k != mid] + [mid]
    home = cut(0, planes_count, 0)
    first = shift(cut(0, planes_count, 1), "uly", 1)
    prevs = [shift(home[1:], "blk", 1)]
    pairs = []
    for k in steps:
        pair = cut(1, planes_count, k)
        pairs.append(shift(after(pair, prevs[0]) if k == mid else pair, "uly", k))
    singles = [shift(after(cut(0, 1, k)[0], pairs[0]), "uly", k) for k in range(2, count)]
    prevs.append(shift(jnp.stack([first[1:]] + pairs[:-1]), "blk", 1))
    prevs += [shift(pairs[-1][i], "blk", 1) for i in range(2)]
    return attend(tuple(range(count)), [home, first], pairs, singles, prevs, tokens * count, width)


def solution(mesh):
    placed = (P(("blk", "uly"), None, None),)
    return jax.shard_map(
        shards,
        mesh=mesh,
        in_specs=placed,
        out_specs=(P("blk", "uly"), P("uly", "blk")),
        check_vma=False,
    )
```

```python
import functools
import math

import jax
import jax.numpy as jnp
from jax import lax
from jax.experimental import pallas as pl
from jax.experimental.pallas import tpu as pltpu
from jax.sharding import PartitionSpec as P

HEAD_DIM = 128
TEMPER = 1.0 / math.sqrt(HEAD_DIM)
SCALE = TEMPER * math.log2(math.e)
CONTRACT = (((1,), (1,)), ((), ()))


def shift(value, axis, steps):
    count = lax.axis_size(axis)
    return lax.ppermute(value, axis, [(i, (i + steps) % count) for i in range(count)])


def after(value, *others):
    return lax.optimization_barrier((value, *others))[0]


def stack(parts):
    return parts[0] if len(parts) == 1 else jnp.concatenate(parts, axis=0)


def own_kernel(order, heads, group, *refs):
    count = len(order)
    fulls = refs[:2]
    pairs = refs[2:count]
    singles = refs[count : 2 * count - 2]
    accum, top_out, total_out = refs[2 * count - 2 :]
    piece = fulls[0].shape[1]
    rows = group * piece

    def queries(k, cols):
        return fulls[k][0, :, cols] if k < 2 else singles[k - 2][:, cols]

    def own(which, cols):
        return stack(
            [ref[1 + which, :, cols] for ref in fulls] + [ref[which, :, cols] for ref in pairs]
        )

    for h in range(heads):
        cols = slice(h * HEAD_DIM, (h + 1) * HEAD_DIM)
        keys, values = own(0, cols), own(1, cols)
        for g in range(count // group):
            query = stack([queries(k, cols) for k in range(g * group, (g + 1) * group)])
            scores = lax.dot_general(query, keys, CONTRACT, preferred_element_type=jnp.float32)
            top = jnp.max(scores, axis=1, keepdims=True)
            weights = jnp.exp2((scores - top) * SCALE)
            total = jnp.sum(weights, axis=1, keepdims=True)
            span = slice(g * rows, (g + 1) * rows)
            accum[span, cols] = jnp.dot(
                weights.astype(jnp.bfloat16), values, preferred_element_type=jnp.float32
            )
            top_out[span, cols] = jnp.broadcast_to(top, (rows, HEAD_DIM))
            total_out[span, cols] = jnp.broadcast_to(total, (rows, HEAD_DIM))


def prev_weights_kernel(order, heads, group, *refs):
    count = len(order)
    me = lax.axis_index("uly")
    fulls = refs[:2]
    singles = refs[2:count]
    prev_home, prev_early, prev_last = refs[count : count + 3]
    accum, top_in, total_in, scaled, inverse, packed, turned, stat = refs[count + 3 :]
    piece = fulls[0].shape[1]
    rows = group * piece

    def rows_of(i):
        k = order[i]
        slot = jnp.where(me < k, me + (count - k), me - k)
        return pl.ds(pl.multiple_of(slot * piece, piece), piece)

    def queries(k, cols):
        return fulls[k][0, :, cols] if k < 2 else singles[k - 2][:, cols]

    lane = lax.broadcasted_iota(jnp.int32, (rows, HEAD_DIM), 1)
    logs = [jnp.zeros((rows, HEAD_DIM), jnp.float32)] * (count // group)
    for h in range(heads):
        cols = slice(h * HEAD_DIM, (h + 1) * HEAD_DIM)
        parts = [prev_early[i, 0, :, cols] for i in range(count - 2)]
        keys = stack([prev_home[0, :, cols]] + parts + [prev_last[:, cols]])
        wide = keys.shape[0]
        for g in range(count // group):
            span = slice(g * rows, (g + 1) * rows)
            query = stack([queries(k, cols) for k in range(g * group, (g + 1) * group)])
            scores = lax.dot_general(query, keys, CONTRACT, preferred_element_type=jnp.float32)
            top, total = top_in[span, cols], total_in[span, cols]
            newtop = jnp.maximum(top, jnp.max(scores, axis=1, keepdims=True))
            spread = jnp.concatenate([newtop] * (wide // HEAD_DIM), axis=1)
            weights = jnp.exp2((scores - spread) * SCALE)
            factor = jnp.exp2((top - newtop) * SCALE)
            total = total * factor + jnp.sum(weights, axis=1, keepdims=True)
            packed[span, h * wide : (h + 1) * wide] = weights.astype(jnp.bfloat16)
            recip = 1.0 / total
            inverse[span, cols] = recip
            scaled[span, cols] = accum[span, cols] * (factor * recip)
            logs[g] = jnp.where(lane == h, newtop * TEMPER + jnp.log(total), logs[g])
    for g in range(count // group):
        for i in range(group):
            stat[rows_of(g * group + i), :] = logs[g][i * piece : (i + 1) * piece]
    turned[...] = stat[...].T[:heads, :]


def prev_values_kernel(order, heads, group, *refs):
    count = len(order)
    me = lax.axis_index("uly")
    prev_home, prev_early, prev_last = refs[:3]
    scaled, inverse, packed, turned, out, log_out, result, sem = refs[3:]
    piece = prev_last.shape[0]
    rows = group * piece

    def rows_of(i):
        k = order[i]
        slot = jnp.where(me < k, me + (count - k), me - k)
        return pl.ds(pl.multiple_of(slot * piece, piece), piece)

    copies = [pltpu.make_async_copy(turned, log_out, sem)]
    copies[0].start()
    for h in range(heads):
        cols = slice(h * HEAD_DIM, (h + 1) * HEAD_DIM)
        parts = [prev_early[i, 1, :, cols] for i in range(count - 2)]
        values = stack([prev_home[1, :, cols]] + parts + [prev_last[:, cols]])
        wide = values.shape[0]
        for g in range(count // group):
            span = slice(g * rows, (g + 1) * rows)
            weights = packed[span, h * wide : (h + 1) * wide]
            added = jnp.dot(weights, values, preferred_element_type=jnp.float32)
            normed = scaled[span, cols] + added * inverse[span, cols]
            for i in range(group):
                result[rows_of(g * group + i), cols] = normed[i * piece : (i + 1) * piece]
        copies.append(pltpu.make_async_copy(result.at[:, cols], out.at[:, cols], sem))
        copies[-1].start()
    for copy in copies:
        copy.wait()


def cost(block_len, width):
    return pl.CostEstimate(
        flops=4 * block_len * block_len * width,
        bytes_accessed=7 * block_len * width,
        transcendentals=block_len * block_len * width // HEAD_DIM,
    )


def attend(order, fulls, pairs, singles, prevs, block_len, width):
    count = len(order)
    heads = width // HEAD_DIM
    group = math.gcd(count, 4)
    in_vmem = pl.BlockSpec(memory_space=pltpu.VMEM)
    whole = jax.ShapeDtypeStruct((block_len, width), jnp.float32)
    running = pl.pallas_call(
        functools.partial(own_kernel, order, heads, group),
        out_shape=(whole, whole, whole),
        in_specs=[in_vmem] * (2 * count - 2),
        out_specs=(in_vmem,) * 3,
        compiler_params=pltpu.CompilerParams(vmem_limit_bytes=24 << 20),
        cost_estimate=cost(block_len, width),
        name="attend_own",
    )(*fulls, *pairs, *singles)
    prev_home, prev_early, last_keys, last_values = prevs
    logs = jax.ShapeDtypeStruct((heads, block_len), jnp.float32)
    scaled, inverse, packed, turned = pl.pallas_call(
        functools.partial(prev_weights_kernel, order, heads, group),
        out_shape=(whole, whole, jax.ShapeDtypeStruct((block_len, heads * block_len), jnp.bfloat16), logs),
        in_specs=[in_vmem] * (count + 6),
        out_specs=(in_vmem,) * 4,
        scratch_shapes=[pltpu.VMEM((block_len, HEAD_DIM), jnp.float32)],
        compiler_params=pltpu.CompilerParams(vmem_limit_bytes=24 << 20),
        cost_estimate=cost(block_len, width),
        name="attend_prev_weights",
    )(*fulls, *singles, prev_home, prev_early, last_keys, *running)
    return pl.pallas_call(
        functools.partial(prev_values_kernel, order, heads, group),
        out_shape=(whole, logs),
        in_specs=[in_vmem] * 7,
        out_specs=(pl.BlockSpec(memory_space=pl.ANY),) * 2,
        scratch_shapes=[pltpu.VMEM((block_len, width), jnp.float32), pltpu.SemaphoreType.DMA(())],
        compiler_params=pltpu.CompilerParams(vmem_limit_bytes=24 << 20),
        cost_estimate=cost(block_len, width),
        name="attend_prev_values",
    )(prev_home, prev_early, last_values, scaled, inverse, packed, turned)


def shards(qkv):
    count = lax.axis_size("uly")
    me = lax.axis_index("uly")
    tokens, planes_count, width = qkv.shape[0], qkv.shape[1], qkv.shape[2] // count
    planes = jnp.transpose(qkv, (1, 0, 2))

    def cut(first, last, k):
        start = jnp.where(me + k < count, me + k, me + k - count) * width
        return lax.dynamic_slice(planes, (first, 0, start), (last - first, tokens, width))

    mid = count // 2
    steps = [k for k in range(2, count) if k != mid] + [mid]
    home = cut(0, planes_count, 0)
    first = shift(cut(0, planes_count, 1), "uly", 1)
    prevs = [shift(home[1:], "blk", 1)]
    pairs = []
    for k in steps:
        pair = cut(1, planes_count, k)
        pairs.append(shift(after(pair, prevs[0]), "uly", k))
    singles = [shift(after(cut(0, 1, k)[0], pairs[0]), "uly", k) for k in range(2, count)]
    prevs.append(shift(jnp.stack([first[1:]] + pairs[:-1]), "blk", 1))
    prevs += [shift(pairs[-1][i], "blk", 1) for i in range(2)]
    return attend(tuple(range(count)), [home, first], pairs, singles, prevs, tokens * count, width)


def solution(mesh):
    placed = (P(("blk", "uly"), None, None),)
    return jax.shard_map(
        shards,
        mesh=mesh,
        in_specs=placed,
        out_specs=(P("blk", "uly"), P("uly", "blk")),
        check_vma=False,
    )
```

```python
import functools
import math

import jax
import jax.numpy as jnp
from jax import lax
from jax.experimental import pallas as pl
from jax.experimental.pallas import tpu as pltpu
from jax.sharding import PartitionSpec as P

HEAD_DIM = 128
TEMPER = 1.0 / math.sqrt(HEAD_DIM)
SCALE = TEMPER * math.log2(math.e)
CONTRACT = (((1,), (1,)), ((), ()))


def shift(value, axis, steps):
    count = lax.axis_size(axis)
    return lax.ppermute(value, axis, [(i, (i + steps) % count) for i in range(count)])


def after(value, *others):
    return lax.optimization_barrier((value, *others))[0]


def stack(parts):
    return parts[0] if len(parts) == 1 else jnp.concatenate(parts, axis=0)


def own_kernel(order, heads, group, *refs):
    count = len(order)
    fulls = refs[:2]
    pairs = refs[2:count]
    singles = refs[count : 2 * count - 2]
    accum, top_out, total_out = refs[2 * count - 2 :]
    piece = fulls[0].shape[1]
    rows = group * piece

    def queries(k, cols):
        return fulls[k][0, :, cols] if k < 2 else singles[k - 2][:, cols]

    def own(which, cols):
        return stack(
            [ref[1 + which, :, cols] for ref in fulls] + [ref[which, :, cols] for ref in pairs]
        )

    for h in range(heads):
        cols = slice(h * HEAD_DIM, (h + 1) * HEAD_DIM)
        keys, values = own(0, cols), own(1, cols)
        for g in range(count // group):
            query = stack([queries(k, cols) for k in range(g * group, (g + 1) * group)])
            scores = lax.dot_general(query, keys, CONTRACT, preferred_element_type=jnp.float32)
            top = jnp.max(scores, axis=1, keepdims=True)
            weights = jnp.exp2((scores - top) * SCALE)
            total = jnp.sum(weights, axis=1, keepdims=True)
            span = slice(g * rows, (g + 1) * rows)
            accum[span, cols] = jnp.dot(
                weights.astype(jnp.bfloat16), values, preferred_element_type=jnp.float32
            )
            top_out[span, cols] = jnp.broadcast_to(top, (rows, HEAD_DIM))
            total_out[span, cols] = jnp.broadcast_to(total, (rows, HEAD_DIM))


def prev_weights_kernel(order, heads, group, *refs):
    count = len(order)
    me = lax.axis_index("uly")
    fulls = refs[:2]
    singles = refs[2:count]
    prev_home, prev_early, prev_last = refs[count : count + 3]
    accum, top_in, total_in, scaled, inverse, packed, turned, stat = refs[count + 3 :]
    piece = fulls[0].shape[1]
    rows = group * piece

    def rows_of(i):
        k = order[i]
        slot = jnp.where(me < k, me + (count - k), me - k)
        return pl.ds(pl.multiple_of(slot * piece, piece), piece)

    def queries(k, cols):
        return fulls[k][0, :, cols] if k < 2 else singles[k - 2][:, cols]

    lane = lax.broadcasted_iota(jnp.int32, (rows, HEAD_DIM), 1)
    logs = [jnp.zeros((rows, HEAD_DIM), jnp.float32)] * (count // group)
    for h in range(heads):
        cols = slice(h * HEAD_DIM, (h + 1) * HEAD_DIM)
        parts = [prev_early[i, 0, :, cols] for i in range(count - 2)]
        keys = stack([prev_home[0, :, cols]] + parts + [prev_last[:, cols]])
        wide = keys.shape[0]
        for g in range(count // group):
            span = slice(g * rows, (g + 1) * rows)
            query = stack([queries(k, cols) for k in range(g * group, (g + 1) * group)])
            scores = lax.dot_general(query, keys, CONTRACT, preferred_element_type=jnp.float32)
            top, total = top_in[span, cols], total_in[span, cols]
            newtop = jnp.maximum(top, jnp.max(scores, axis=1, keepdims=True))
            spread = jnp.concatenate([newtop] * (wide // HEAD_DIM), axis=1)
            weights = jnp.exp2((scores - spread) * SCALE)
            factor = jnp.exp2((top - newtop) * SCALE)
            total = total * factor + jnp.sum(weights, axis=1, keepdims=True)
            packed[span, h * wide : (h + 1) * wide] = weights.astype(jnp.bfloat16)
            recip = 1.0 / total
            inverse[span, cols] = recip
            scaled[span, cols] = accum[span, cols] * (factor * recip)
            logs[g] = jnp.where(lane == h, newtop * TEMPER + jnp.log(total), logs[g])
    for g in range(count // group):
        for i in range(group):
            stat[rows_of(g * group + i), :] = logs[g][i * piece : (i + 1) * piece]
    turned[...] = stat[...].T[:heads, :]


def prev_values_kernel(order, heads, group, *refs):
    count = len(order)
    me = lax.axis_index("uly")
    prev_home, prev_early, prev_last = refs[:3]
    scaled, inverse, packed, turned, out, log_out, result, sem = refs[3:]
    piece = prev_last.shape[0]
    rows = group * piece

    def rows_of(i):
        k = order[i]
        slot = jnp.where(me < k, me + (count - k), me - k)
        return pl.ds(pl.multiple_of(slot * piece, piece), piece)

    copies = [pltpu.make_async_copy(turned, log_out, sem)]
    copies[0].start()
    for h in range(heads):
        cols = slice(h * HEAD_DIM, (h + 1) * HEAD_DIM)
        parts = [prev_early[i, 1, :, cols] for i in range(count - 2)]
        values = stack([prev_home[1, :, cols]] + parts + [prev_last[:, cols]])
        wide = values.shape[0]
        for g in range(count // group):
            span = slice(g * rows, (g + 1) * rows)
            weights = packed[span, h * wide : (h + 1) * wide]
            added = jnp.dot(weights, values, preferred_element_type=jnp.float32)
            normed = scaled[span, cols] + added * inverse[span, cols]
            for i in range(group):
                result[rows_of(g * group + i), cols] = normed[i * piece : (i + 1) * piece]
        copies.append(pltpu.make_async_copy(result.at[:, cols], out.at[:, cols], sem))
        copies[-1].start()
    for copy in copies:
        copy.wait()


def cost(block_len, width):
    return pl.CostEstimate(
        flops=4 * block_len * block_len * width,
        bytes_accessed=7 * block_len * width,
        transcendentals=block_len * block_len * width // HEAD_DIM,
    )


def attend(order, fulls, pairs, singles, prevs, block_len, width):
    count = len(order)
    heads = width // HEAD_DIM
    group = math.gcd(count, 4)
    in_vmem = pl.BlockSpec(memory_space=pltpu.VMEM)
    whole = jax.ShapeDtypeStruct((block_len, width), jnp.float32)
    running = pl.pallas_call(
        functools.partial(own_kernel, order, heads, group),
        out_shape=(whole, whole, whole),
        in_specs=[in_vmem] * (2 * count - 2),
        out_specs=(in_vmem,) * 3,
        compiler_params=pltpu.CompilerParams(vmem_limit_bytes=24 << 20),
        cost_estimate=cost(block_len, width),
        name="attend_own",
    )(*fulls, *pairs, *singles)
    prev_home, prev_early, last_keys, last_values = prevs
    logs = jax.ShapeDtypeStruct((heads, block_len), jnp.float32)
    scaled, inverse, packed, turned = pl.pallas_call(
        functools.partial(prev_weights_kernel, order, heads, group),
        out_shape=(whole, whole, jax.ShapeDtypeStruct((block_len, heads * block_len), jnp.bfloat16), logs),
        in_specs=[in_vmem] * (count + 6),
        out_specs=(in_vmem,) * 4,
        scratch_shapes=[pltpu.VMEM((block_len, HEAD_DIM), jnp.float32)],
        compiler_params=pltpu.CompilerParams(vmem_limit_bytes=24 << 20),
        cost_estimate=cost(block_len, width),
        name="attend_prev_weights",
    )(*fulls, *singles, prev_home, prev_early, last_keys, *running)
    return pl.pallas_call(
        functools.partial(prev_values_kernel, order, heads, group),
        out_shape=(whole, logs),
        in_specs=[in_vmem] * 7,
        out_specs=(pl.BlockSpec(memory_space=pl.ANY),) * 2,
        scratch_shapes=[pltpu.VMEM((block_len, width), jnp.float32), pltpu.SemaphoreType.DMA(())],
        compiler_params=pltpu.CompilerParams(vmem_limit_bytes=24 << 20),
        cost_estimate=cost(block_len, width),
        name="attend_prev_values",
    )(prev_home, prev_early, last_values, scaled, inverse, packed, turned)


def shards(qkv):
    count = lax.axis_size("uly")
    me = lax.axis_index("uly")
    tokens, planes_count, width = qkv.shape[0], qkv.shape[1], qkv.shape[2] // count
    planes = jnp.transpose(qkv, (1, 0, 2))

    def cut(first, last, k):
        start = jnp.where(me + k < count, me + k, me + k - count) * width
        return lax.dynamic_slice(planes, (first, 0, start), (last - first, tokens, width))

    mid = count // 2
    steps = [k for k in range(2, count) if k != mid] + [mid]
    home = cut(0, planes_count, 0)
    first = shift(cut(0, planes_count, 1), "uly", 1)
    prevs = [shift(home[1:], "blk", 1)]
    pairs = []
    for k in steps:
        pair = cut(1, planes_count, k)
        pairs.append(shift(after(pair, prevs[0]) if k != mid else after(pair, prevs[0], first), "uly", k))
    singles = [shift(after(cut(0, 1, k)[0], first), "uly", k) for k in range(2, count)]
    prevs.append(shift(jnp.stack([first[1:]] + pairs[:-1]), "blk", 1))
    prevs += [shift(pairs[-1][i], "blk", 1) for i in range(2)]
    return attend(tuple(range(count)), [home, first], pairs, singles, prevs, tokens * count, width)


def solution(mesh):
    placed = (P(("blk", "uly"), None, None),)
    return jax.shard_map(
        shards,
        mesh=mesh,
        in_specs=placed,
        out_specs=(P("blk", "uly"), P("uly", "blk")),
        check_vma=False,
    )
```

```python
import functools
import math

import jax
import jax.numpy as jnp
from jax import lax
from jax.experimental import pallas as pl
from jax.experimental.pallas import tpu as pltpu
from jax.sharding import PartitionSpec as P

HEAD_DIM = 128
TEMPER = 1.0 / math.sqrt(HEAD_DIM)
SCALE = TEMPER * math.log2(math.e)
CONTRACT = (((1,), (1,)), ((), ()))


def shift(value, axis, steps):
    count = lax.axis_size(axis)
    return lax.ppermute(value, axis, [(i, (i + steps) % count) for i in range(count)])


def after(value, *others):
    return lax.optimization_barrier((value, *others))[0]


def stack(parts):
    return parts[0] if len(parts) == 1 else jnp.concatenate(parts, axis=0)


def own_kernel(order, heads, group, *refs):
    count = len(order)
    fulls = refs[:2]
    pairs = refs[2:count]
    singles = refs[count : 2 * count - 2]
    accum, top_out, total_out = refs[2 * count - 2 :]
    piece = fulls[0].shape[1]
    rows = group * piece

    def queries(k, cols):
        return fulls[k][0, :, cols] if k < 2 else singles[k - 2][:, cols]

    def own(which, cols):
        return stack(
            [ref[1 + which, :, cols] for ref in fulls] + [ref[which, :, cols] for ref in pairs]
        )

    for h in range(heads):
        cols = slice(h * HEAD_DIM, (h + 1) * HEAD_DIM)
        keys, values = own(0, cols), own(1, cols)
        for g in range(count // group):
            query = stack([queries(k, cols) for k in range(g * group, (g + 1) * group)])
            scores = lax.dot_general(query, keys, CONTRACT, preferred_element_type=jnp.float32)
            top = jnp.max(scores, axis=1, keepdims=True)
            weights = jnp.exp2((scores - top) * SCALE)
            total = jnp.sum(weights, axis=1, keepdims=True)
            span = slice(g * rows, (g + 1) * rows)
            accum[span, cols] = jnp.dot(
                weights.astype(jnp.bfloat16), values, preferred_element_type=jnp.float32
            )
            top_out[span, cols] = jnp.broadcast_to(top, (rows, HEAD_DIM))
            total_out[span, cols] = jnp.broadcast_to(total, (rows, HEAD_DIM))


def prev_weights_kernel(order, heads, group, *refs):
    count = len(order)
    me = lax.axis_index("uly")
    fulls = refs[:2]
    singles = refs[2:count]
    prev_home, prev_early, prev_last = refs[count : count + 3]
    accum, top_in, total_in, scaled, inverse, packed, turned, stat = refs[count + 3 :]
    piece = fulls[0].shape[1]
    rows = group * piece

    def rows_of(i):
        k = order[i]
        slot = jnp.where(me < k, me + (count - k), me - k)
        return pl.ds(pl.multiple_of(slot * piece, piece), piece)

    def queries(k, cols):
        return fulls[k][0, :, cols] if k < 2 else singles[k - 2][:, cols]

    lane = lax.broadcasted_iota(jnp.int32, (rows, HEAD_DIM), 1)
    logs = [jnp.zeros((rows, HEAD_DIM), jnp.float32)] * (count // group)
    for h in range(heads):
        cols = slice(h * HEAD_DIM, (h + 1) * HEAD_DIM)
        parts = [prev_early[i, 0, :, cols] for i in range(count - 2)]
        keys = stack([prev_home[0, :, cols]] + parts + [prev_last[:, cols]])
        wide = keys.shape[0]
        for g in range(count // group):
            span = slice(g * rows, (g + 1) * rows)
            query = stack([queries(k, cols) for k in range(g * group, (g + 1) * group)])
            scores = lax.dot_general(query, keys, CONTRACT, preferred_element_type=jnp.float32)
            top, total = top_in[span, cols], total_in[span, cols]
            newtop = jnp.maximum(top, jnp.max(scores, axis=1, keepdims=True))
            spread = jnp.concatenate([newtop] * (wide // HEAD_DIM), axis=1)
            weights = jnp.exp2((scores - spread) * SCALE)
            factor = jnp.exp2((top - newtop) * SCALE)
            total = total * factor + jnp.sum(weights, axis=1, keepdims=True)
            packed[span, h * wide : (h + 1) * wide] = weights.astype(jnp.bfloat16)
            recip = 1.0 / total
            inverse[span, cols] = recip
            scaled[span, cols] = accum[span, cols] * (factor * recip)
            logs[g] = jnp.where(lane == h, newtop * TEMPER + jnp.log(total), logs[g])
    for g in range(count // group):
        for i in range(group):
            stat[rows_of(g * group + i), :] = logs[g][i * piece : (i + 1) * piece]
    turned[...] = stat[...].T[:heads, :]


def prev_values_kernel(order, heads, group, *refs):
    count = len(order)
    me = lax.axis_index("uly")
    prev_home, prev_early, prev_last = refs[:3]
    scaled, inverse, packed, turned, out, log_out, result, sem = refs[3:]
    piece = prev_last.shape[0]
    rows = group * piece

    def rows_of(i):
        k = order[i]
        slot = jnp.where(me < k, me + (count - k), me - k)
        return pl.ds(pl.multiple_of(slot * piece, piece), piece)

    copies = [pltpu.make_async_copy(turned, log_out, sem)]
    copies[0].start()
    for h in range(heads):
        cols = slice(h * HEAD_DIM, (h + 1) * HEAD_DIM)
        parts = [prev_early[i, 1, :, cols] for i in range(count - 2)]
        values = stack([prev_home[1, :, cols]] + parts + [prev_last[:, cols]])
        wide = values.shape[0]
        for g in range(count // group):
            span = slice(g * rows, (g + 1) * rows)
            weights = packed[span, h * wide : (h + 1) * wide]
            added = jnp.dot(weights, values, preferred_element_type=jnp.float32)
            normed = scaled[span, cols] + added * inverse[span, cols]
            for i in range(group):
                place = rows_of(g * group + i)
                result[place, cols] = normed[i * piece : (i + 1) * piece]
                copies.append(pltpu.make_async_copy(result.at[place, cols], out.at[place, cols], sem))
                copies[-1].start()
    for copy in copies:
        copy.wait()


def cost(block_len, width):
    return pl.CostEstimate(
        flops=4 * block_len * block_len * width,
        bytes_accessed=7 * block_len * width,
        transcendentals=block_len * block_len * width // HEAD_DIM,
    )


def attend(order, fulls, pairs, singles, prevs, block_len, width):
    count = len(order)
    heads = width // HEAD_DIM
    group = math.gcd(count, 4)
    in_vmem = pl.BlockSpec(memory_space=pltpu.VMEM)
    whole = jax.ShapeDtypeStruct((block_len, width), jnp.float32)
    running = pl.pallas_call(
        functools.partial(own_kernel, order, heads, group),
        out_shape=(whole, whole, whole),
        in_specs=[in_vmem] * (2 * count - 2),
        out_specs=(in_vmem,) * 3,
        compiler_params=pltpu.CompilerParams(vmem_limit_bytes=24 << 20),
        cost_estimate=cost(block_len, width),
        name="attend_own",
    )(*fulls, *pairs, *singles)
    prev_home, prev_early, last_keys, last_values = prevs
    logs = jax.ShapeDtypeStruct((heads, block_len), jnp.float32)
    scaled, inverse, packed, turned = pl.pallas_call(
        functools.partial(prev_weights_kernel, order, heads, group),
        out_shape=(whole, whole, jax.ShapeDtypeStruct((block_len, heads * block_len), jnp.bfloat16), logs),
        in_specs=[in_vmem] * (count + 6),
        out_specs=(in_vmem,) * 4,
        scratch_shapes=[pltpu.VMEM((block_len, HEAD_DIM), jnp.float32)],
        compiler_params=pltpu.CompilerParams(vmem_limit_bytes=24 << 20),
        cost_estimate=cost(block_len, width),
        name="attend_prev_weights",
    )(*fulls, *singles, prev_home, prev_early, last_keys, *running)
    return pl.pallas_call(
        functools.partial(prev_values_kernel, order, heads, group),
        out_shape=(whole, logs),
        in_specs=[in_vmem] * 7,
        out_specs=(pl.BlockSpec(memory_space=pl.ANY),) * 2,
        scratch_shapes=[pltpu.VMEM((block_len, width), jnp.float32), pltpu.SemaphoreType.DMA(())],
        compiler_params=pltpu.CompilerParams(vmem_limit_bytes=24 << 20),
        cost_estimate=cost(block_len, width),
        name="attend_prev_values",
    )(prev_home, prev_early, last_values, scaled, inverse, packed, turned)


def shards(qkv):
    count = lax.axis_size("uly")
    me = lax.axis_index("uly")
    tokens, planes_count, width = qkv.shape[0], qkv.shape[1], qkv.shape[2] // count
    planes = jnp.transpose(qkv, (1, 0, 2))

    def cut(first, last, k):
        start = jnp.where(me + k < count, me + k, me + k - count) * width
        return lax.dynamic_slice(planes, (first, 0, start), (last - first, tokens, width))

    mid = count // 2
    steps = [k for k in range(2, count) if k != mid] + [mid]
    home = cut(0, planes_count, 0)
    first = shift(cut(0, planes_count, 1), "uly", 1)
    prevs = [shift(home[1:], "blk", 1)]
    pairs = []
    for k in steps:
        pair = cut(1, planes_count, k)
        pairs.append(shift(after(pair, prevs[0]), "uly", k))
    singles = [shift(after(cut(0, 1, k)[0], first), "uly", k) for k in range(2, count)]
    prevs.append(shift(jnp.stack([first[1:]] + pairs[:-1]), "blk", 1))
    prevs += [shift(pairs[-1][i], "blk", 1) for i in range(2)]
    return attend(tuple(range(count)), [home, first], pairs, singles, prevs, tokens * count, width)


def solution(mesh):
    placed = (P(("blk", "uly"), None, None),)
    return jax.shard_map(
        shards,
        mesh=mesh,
        in_specs=placed,
        out_specs=(P("blk", "uly"), P("uly", "blk")),
        check_vma=False,
    )
```

```python
import functools
import math

import jax
import jax.numpy as jnp
from jax import lax
from jax.experimental import pallas as pl
from jax.experimental.pallas import tpu as pltpu
from jax.sharding import PartitionSpec as P

HEAD_DIM = 128
TEMPER = 1.0 / math.sqrt(HEAD_DIM)
SCALE = TEMPER * math.log2(math.e)
CONTRACT = (((1,), (1,)), ((), ()))


def shift(value, axis, steps):
    count = lax.axis_size(axis)
    return lax.ppermute(value, axis, [(i, (i + steps) % count) for i in range(count)])


def after(value, *others):
    return lax.optimization_barrier((value, *others))[0]


def stack(parts):
    return parts[0] if len(parts) == 1 else jnp.concatenate(parts, axis=0)


def own_kernel(order, heads, group, *refs):
    count = len(order)
    fulls = refs[:2]
    pairs = refs[2:count]
    singles = refs[count : 2 * count - 2]
    accum, top_out, total_out = refs[2 * count - 2 :]
    piece = fulls[0].shape[1]
    rows = group * piece

    def queries(k, cols):
        return fulls[k][0, :, cols] if k < 2 else singles[k - 2][:, cols]

    def own(which, cols):
        return stack(
            [ref[1 + which, :, cols] for ref in fulls] + [ref[which, :, cols] for ref in pairs]
        )

    for h in range(heads):
        cols = slice(h * HEAD_DIM, (h + 1) * HEAD_DIM)
        keys, values = own(0, cols), own(1, cols)
        for g in range(count // group):
            query = stack([queries(k, cols) for k in range(g * group, (g + 1) * group)])
            scores = lax.dot_general(query, keys, CONTRACT, preferred_element_type=jnp.float32)
            top = jnp.max(scores, axis=1, keepdims=True)
            weights = jnp.exp2((scores - top) * SCALE)
            total = jnp.sum(weights, axis=1, keepdims=True)
            span = slice(g * rows, (g + 1) * rows)
            accum[span, cols] = jnp.dot(
                weights.astype(jnp.bfloat16), values, preferred_element_type=jnp.float32
            )
            top_out[span, cols] = jnp.broadcast_to(top, (rows, HEAD_DIM))
            total_out[span, cols] = jnp.broadcast_to(total, (rows, HEAD_DIM))


def prev_weights_kernel(order, heads, group, *refs):
    count = len(order)
    me = lax.axis_index("uly")
    fulls = refs[:2]
    singles = refs[2:count]
    prev_home, prev_early, prev_last = refs[count : count + 3]
    accum, top_in, total_in, scaled, inverse, packed, turned, stat = refs[count + 3 :]
    piece = fulls[0].shape[1]
    rows = group * piece

    def rows_of(i):
        k = order[i]
        slot = jnp.where(me < k, me + (count - k), me - k)
        return pl.ds(pl.multiple_of(slot * piece, piece), piece)

    def queries(k, cols):
        return fulls[k][0, :, cols] if k < 2 else singles[k - 2][:, cols]

    lane = lax.broadcasted_iota(jnp.int32, (rows, HEAD_DIM), 1)
    logs = [jnp.zeros((rows, HEAD_DIM), jnp.float32)] * (count // group)
    for h in range(heads):
        cols = slice(h * HEAD_DIM, (h + 1) * HEAD_DIM)
        parts = [prev_early[i, 0, :, cols] for i in range(count - 2)]
        keys = stack([prev_home[0, :, cols]] + parts + [prev_last[:, cols]])
        wide = keys.shape[0]
        for g in range(count // group):
            span = slice(g * rows, (g + 1) * rows)
            query = stack([queries(k, cols) for k in range(g * group, (g + 1) * group)])
            scores = lax.dot_general(query, keys, CONTRACT, preferred_element_type=jnp.float32)
            top, total = top_in[span, cols], total_in[span, cols]
            newtop = jnp.maximum(top, jnp.max(scores, axis=1, keepdims=True))
            spread = jnp.concatenate([newtop] * (wide // HEAD_DIM), axis=1)
            weights = jnp.exp2((scores - spread) * SCALE)
            factor = jnp.exp2((top - newtop) * SCALE)
            total = total * factor + jnp.sum(weights, axis=1, keepdims=True)
            packed[span, h * wide : (h + 1) * wide] = weights.astype(jnp.bfloat16)
            recip = 1.0 / total
            inverse[span, cols] = recip
            scaled[span, cols] = accum[span, cols] * (factor * recip)
            logs[g] = jnp.where(lane == h, newtop * TEMPER + jnp.log(total), logs[g])
    for g in range(count // group):
        for i in range(group):
            stat[rows_of(g * group + i), :] = logs[g][i * piece : (i + 1) * piece]
    turned[...] = stat[...].T[:heads, :]


def prev_values_kernel(order, heads, group, *refs):
    count = len(order)
    me = lax.axis_index("uly")
    prev_home, prev_early, prev_last = refs[:3]
    scaled, inverse, packed, turned, out, log_out, result, sem = refs[3:]
    piece = prev_last.shape[0]
    rows = group * piece

    def rows_of(i):
        k = order[i]
        slot = jnp.where(me < k, me + (count - k), me - k)
        return pl.ds(pl.multiple_of(slot * piece, piece), piece)

    copies = [pltpu.make_async_copy(turned, log_out, sem)]
    copies[0].start()
    for h in range(heads):
        cols = slice(h * HEAD_DIM, (h + 1) * HEAD_DIM)
        parts = [prev_early[i, 1, :, cols] for i in range(count - 2)]
        values = stack([prev_home[1, :, cols]] + parts + [prev_last[:, cols]])
        wide = values.shape[0]
        for g in range(count // group):
            span = slice(g * rows, (g + 1) * rows)
            weights = packed[span, h * wide : (h + 1) * wide]
            added = jnp.dot(weights, values, preferred_element_type=jnp.float32)
            normed = scaled[span, cols] + added * inverse[span, cols]
            for i in range(group):
                result[rows_of(g * group + i), cols] = normed[i * piece : (i + 1) * piece]
        copies.append(pltpu.make_async_copy(result.at[:, cols], out.at[:, cols], sem))
        copies[-1].start()
    for copy in copies:
        copy.wait()


def cost(block_len, width):
    return pl.CostEstimate(
        flops=4 * block_len * block_len * width,
        bytes_accessed=7 * block_len * width,
        transcendentals=block_len * block_len * width // HEAD_DIM,
    )


def attend(order, fulls, pairs, singles, prevs, block_len, width):
    count = len(order)
    heads = width // HEAD_DIM
    group = math.gcd(count, 4)
    in_vmem = pl.BlockSpec(memory_space=pltpu.VMEM)
    whole = jax.ShapeDtypeStruct((block_len, width), jnp.float32)
    running = pl.pallas_call(
        functools.partial(own_kernel, order, heads, group),
        out_shape=(whole, whole, whole),
        in_specs=[in_vmem] * (2 * count - 2),
        out_specs=(in_vmem,) * 3,
        compiler_params=pltpu.CompilerParams(vmem_limit_bytes=24 << 20),
        cost_estimate=cost(block_len, width),
        name="attend_own",
    )(*fulls, *pairs, *singles)
    prev_home, prev_early, last_keys, last_values = prevs
    logs = jax.ShapeDtypeStruct((heads, block_len), jnp.float32)
    scaled, inverse, packed, turned = pl.pallas_call(
        functools.partial(prev_weights_kernel, order, heads, group),
        out_shape=(whole, whole, jax.ShapeDtypeStruct((block_len, heads * block_len), jnp.bfloat16), logs),
        in_specs=[in_vmem] * (count + 6),
        out_specs=(in_vmem,) * 4,
        scratch_shapes=[pltpu.VMEM((block_len, HEAD_DIM), jnp.float32)],
        compiler_params=pltpu.CompilerParams(vmem_limit_bytes=24 << 20),
        cost_estimate=cost(block_len, width),
        name="attend_prev_weights",
    )(*fulls, *singles, prev_home, prev_early, last_keys, *running)
    return pl.pallas_call(
        functools.partial(prev_values_kernel, order, heads, group),
        out_shape=(whole, logs),
        in_specs=[in_vmem] * 7,
        out_specs=(pl.BlockSpec(memory_space=pl.ANY),) * 2,
        scratch_shapes=[pltpu.VMEM((block_len, width), jnp.float32), pltpu.SemaphoreType.DMA(())],
        compiler_params=pltpu.CompilerParams(vmem_limit_bytes=24 << 20),
        cost_estimate=cost(block_len, width),
        name="attend_prev_values",
    )(prev_home, prev_early, last_values, scaled, inverse, packed, turned)


def shards(qkv):
    count = lax.axis_size("uly")
    me = lax.axis_index("uly")
    tokens, planes_count, width = qkv.shape[0], qkv.shape[1], qkv.shape[2] // count
    planes = jnp.transpose(qkv, (1, 0, 2))

    def cut(first, last, k):
        start = jnp.where(me + k < count, me + k, me + k - count) * width
        return lax.dynamic_slice(planes, (first, 0, start), (last - first, tokens, width))

    mid = count // 2
    steps = [k for k in range(2, count) if k != mid] + [mid]
    home = cut(0, planes_count, 0)
    first = shift(cut(0, planes_count, 1), "uly", 1)
    prevs = [shift(home[1:], "blk", 1)]
    pairs = []
    for k in steps:
        pair = cut(1, planes_count, k)
        pairs.append(shift(after(pair, prevs[0]) if k != mid else after(pair, prevs[0], first), "uly", k))
    singles = [shift(after(cut(0, 1, k)[0], pairs[0]), "uly", k) for k in range(2, count)]
    prevs.append(shift(jnp.stack([first[1:]] + pairs[:-1]), "blk", 1))
    prevs += [shift(pairs[-1][i], "blk", 1) for i in range(2)]
    return attend(tuple(range(count)), [home, first], pairs, singles, prevs, tokens * count, width)


def solution(mesh):
    placed = (P(("blk", "uly"), None, None),)
    return jax.shard_map(
        shards,
        mesh=mesh,
        in_specs=placed,
        out_specs=(P("blk", "uly"), P("uly", "blk")),
        check_vma=False,
    )
```
